32 devices in a mesh: groups: 2 (over x), queue: 16 (over z, y, core).
Axes of the slice: x: 2, y: 2, z: 4, core: 2. Of those that a mesh axis runs over, the one named last changes fastest.
Arguments:
- query: bfloat16 [32, 768, 2560], P(('groups', 'queue')), parts along dimension 0, may hold values from -6 to 6
- keys: bfloat16 [32, 768, 2560], P(('groups', 'queue')), parts along dimension 0, may hold values from -6 to 6
- values: bfloat16 [32, 768, 2560], P(('groups', 'queue')), parts along dimension 0, may hold values from -6 to 6
- gate_table: float32 [50, 2, 2560], replicated, may hold values from 0.5 to 2
- levels: int32 [32], P('groups'), parts along dimension 0, may hold values from 0 to 49
- window: int32 [32], P('groups'), parts along dimension 0, may hold values from 0 to 2, as said below
- queue_head: int32 [2], P('groups'), parts along dimension 0, may hold values from 1 to 15
Outputs:
- attended: bfloat16 [32, 768, 2560], P(('groups', 'queue')), parts along dimension 0
The draws below stay inside these ranges and needn't reach their ends.
There are 2 independent parts, one for each index of `groups`. The reference program is written for one: setup_inputs(seed, part) draws one part's arguments, and reference() takes and returns one part's arrays. A program takes and returns all parts, laid end to end along the dimension named above; an argument that names none is the same for every part. Nothing has to cross between parts.
Inputs may be any that keep to these rules, and one draw needn't show every extreme that they name: `window`: at least one slot has width 2.
All inputs are finite; a program needn't handle non-finite values.
Results may differ from the reference program's by a relative error of at most 0.008.
Values may be sent and summed in bfloat16 or wider, within the bound.
No kernel may reach another device: no remote copies, remote signals or barrier semaphores. Data moves between devices by JAX's collectives and lax.ppermute only.
A program may use at most 192 MiB of HBM per device.

```python
import math
import jax
import jax.numpy as jnp
from jax import lax

HEADS = 20
HEAD_DIM = 128
FRAME_TOK = 768
REACH = 2
LEVELS = 50
SLOTS = 16
D = 2560


def draw_pair(key, which):
    shape = (SLOTS, FRAME_TOK, HEADS, HEAD_DIM)
    result = jnp.clip(jax.random.normal(jax.random.fold_in(key, 3 + which), shape, jnp.float32), -6.0, 6.0)
    return result.reshape(SLOTS, FRAME_TOK, HEADS * HEAD_DIM).astype(jnp.bfloat16)


def draw_query(key, part):
    return draw_pair(key, 0)


def draw_keys(key, part):
    return draw_pair(key, 1)


def draw_window(key, part):
    drawn = jax.random.randint(jax.random.fold_in(key, 29), (SLOTS,), 0, REACH + 1)
    return jnp.where(jnp.arange(SLOTS) == 0, REACH, drawn).astype(jnp.int32)


def place_ends(values, stream_key, low, top_value):
    longest = values.shape.index(max(values.shape))
    spots = []
    for shift in (0, 1):
        where = [jax.random.randint(jax.random.fold_in(stream_key, axis), (), 0, length) for axis, length in enumerate(values.shape)]
        where[longest] = (where[longest] + shift) % values.shape[longest]
        spots.append(tuple(where))
    return values.at[spots[0]].set(low).at[spots[1]].set(top_value)


def block_levels(rng, shape, shards, smallest, largest):
    gain = 1.0
    for axis_at, shards_of in shards:
        draws = jax.random.uniform(jax.random.fold_in(jax.random.fold_in(rng, 6), axis_at), (shards_of,), jnp.float32, smallest / len(shards), largest / len(shards))
        gain = gain * jnp.repeat(jnp.exp(draws), shape[axis_at] // shards_of).reshape((-1,) + (1,) * (len(shape) - 1 - axis_at))
    return gain


def scatter_about(stream_key, extent, width, bound, shards=(), kind=jnp.bfloat16):
    values = width * jax.random.normal(stream_key, extent, jnp.float32)
    if shards:
        values = values * block_levels(stream_key, extent, shards, -0.22, 0.18)
    return jnp.clip(values, -bound, bound).astype(kind)


def setup_inputs(seed: int = 0, part: int = 0) -> dict:
    key_list = jax.random.split(jax.random.key(seed), 8)
    part_splits = jax.random.split(jax.random.fold_in(key_list[7], part), 8)
    query = draw_query(jax.random.fold_in(jax.random.fold_in(key_list[7], part), 71), part)
    keys = draw_keys(jax.random.fold_in(jax.random.fold_in(key_list[7], part), 71), part)
    values = scatter_about(part_splits[2], (SLOTS, FRAME_TOK, D), 1.0, 6.0, ((0, 16),))
    gate_table = jnp.clip(jnp.exp(jax.random.uniform(key_list[3], (LEVELS, 2, D), jnp.float32, math.log(0.5), math.log(2.0))), 0.5, 2.0)
    levels = place_ends(jax.random.randint(part_splits[4], (SLOTS,), 0, LEVELS), jax.random.fold_in(part_splits[4], 1), 0, LEVELS - 1).astype(jnp.int32)
    window = draw_window(jax.random.fold_in(jax.random.fold_in(key_list[7], part), 71), part)
    queue_head = jax.random.randint(part_splits[6], (1,), 1, SLOTS).astype(jnp.int32)
    return {"query": query, "keys": keys, "values": values, "gate_table": gate_table, "levels": levels, "window": window, "queue_head": queue_head}


def spatial_frame(query_f, keys_f, values_f):
    head_groups = math.gcd(HEADS, 4)
    per_group = HEADS // head_groups
    span_cols = per_group * HEAD_DIM
    score_scale = 1.0 / math.sqrt(HEAD_DIM)
    pieces = []
    for group_index in range(head_groups):
        lower = group_index * span_cols
        q_part = query_f[:, lower:lower + span_cols].reshape(FRAME_TOK, per_group, HEAD_DIM).astype(jnp.float32)
        k_part = keys_f[:, lower:lower + span_cols].reshape(FRAME_TOK, per_group, HEAD_DIM).astype(jnp.float32)
        v_part = values_f[:, lower:lower + span_cols].reshape(FRAME_TOK, per_group, HEAD_DIM).astype(jnp.float32)
        scores = jnp.einsum('qhd,khd->hqk', q_part, k_part) * score_scale
        top_score = lax.optimization_barrier(jnp.max(scores, axis=-1, keepdims=True))
        expd = jnp.exp(scores - top_score)
        weights = (expd / lax.optimization_barrier(jnp.sum(expd, axis=-1, keepdims=True))).astype(jnp.bfloat16)
        mixed_part = jnp.einsum('hqk,khd->qhd', weights.astype(jnp.float32), v_part)
        pieces.append(mixed_part.reshape(FRAME_TOK, span_cols))
    return jnp.concatenate(pieces, axis=1)

def reference(query, keys, values, gate_table, levels, window, queue_head):
    spatial = lax.map(lambda trio: spatial_frame(trio[0], trio[1], trio[2]), (query, keys, values))
    slot_count = query.shape[0]
    score_scale = 1.0 / math.sqrt(HEAD_DIM)
    positions = (jnp.arange(slot_count, dtype=jnp.int32) - queue_head[0]) % slot_count
    query_four = query.reshape(slot_count, FRAME_TOK, HEADS, HEAD_DIM).astype(jnp.float32)
    score_list = []
    value_list = []
    for offset in range(-REACH, REACH + 1):
        keys_near = jnp.roll(keys, -offset, axis=0).reshape(slot_count, FRAME_TOK, HEADS, HEAD_DIM).astype(jnp.float32)
        values_near = jnp.roll(values, -offset, axis=0).reshape(slot_count, FRAME_TOK, HEADS, HEAD_DIM)
        scores = jnp.einsum('sthd,sthd->sth', query_four, keys_near) * score_scale
        valid = (abs(offset) <= window) & (positions + offset >= 0) & (positions + offset < slot_count)
        score_list.append(jnp.where(valid[:, None, None], scores, -1e+30))
        value_list.append(values_near)
    stacked = jnp.stack(score_list)
    top_score = lax.optimization_barrier(jnp.max(stacked, axis=0))
    expd = jnp.exp(stacked - top_score[None])
    weights = expd / lax.optimization_barrier(jnp.sum(expd, axis=0))[None]
    temporal = jnp.zeros((slot_count, FRAME_TOK, HEADS, HEAD_DIM), jnp.float32)
    for index in range(len(value_list)):
        temporal = temporal + weights[index][..., None] * value_list[index].astype(jnp.float32)
    temporal = temporal.astype(jnp.bfloat16).reshape(slot_count, FRAME_TOK, D)
    gates = gate_table[levels]
    blended = gates[:, 0][:, None, :] * spatial + gates[:, 1][:, None, :] * temporal.astype(jnp.float32)
    return blended.astype(jnp.bfloat16)
```

```python
import functools
import math

import jax
import jax.numpy as jnp
from jax import lax
from jax.experimental import pallas as pl
from jax.experimental.pallas import tpu as pltpu
from jax.sharding import PartitionSpec as P

HEADS = 20
HEAD_DIM = 128
REACH = 2
CHUNKS = 6
HEADS_PER_CALL = 4
SCALE = 1.0 / math.sqrt(HEAD_DIM)


def moved(value, axis, where_to):
    count = lax.axis_size(axis)
    return lax.ppermute(value, axis, [(source, where_to(source) % count) for source in range(count)])


def other_core(index):
    return index ^ 1


def pair_chip(index):
    return index ^ 2


def onward(index):
    return index - 4 if index & 2 else index + 4


def pack_kernel(core_ref, k_mine, v_mine, k_other, v_other, mine_ref, other_ref):
    mine_ref[0] = k_mine[...]
    mine_ref[1] = v_mine[...]
    other_ref[0] = k_other[...]
    other_ref[1] = v_other[...]


def pack(core, keys, values, chunk, rows):
    half = keys.shape[1] // 2
    mine = pl.BlockSpec((rows, half), lambda i, c: (chunk, c[0]))
    other = pl.BlockSpec((rows, half), lambda i, c: (chunk, 1 - c[0]))
    whole = pl.BlockSpec((2, rows, half), lambda i, c: (0, 0, 0))
    shape = jax.ShapeDtypeStruct((2, rows, half), keys.dtype)
    return pl.pallas_call(
        pack_kernel,
        grid_spec=pltpu.PrefetchScalarGridSpec(
            num_scalar_prefetch=1,
            grid=(1,),
            in_specs=[mine, mine, other, other],
            out_specs=[whole, whole],
        ),
        out_shape=[shape, shape],
        cost_estimate=pl.CostEstimate(
            flops=0, bytes_accessed=16 * rows * half, transcendentals=0
        ),
        name="pack",
    )(core, keys, values, keys, values)


def half_kernel(core_ref, x_ref, o_ref):
    o_ref[...] = x_ref[...]


def other_half(core, x):
    rows, half = x.shape[0], x.shape[1] // 2
    return pl.pallas_call(
        half_kernel,
        grid_spec=pltpu.PrefetchScalarGridSpec(
            num_scalar_prefetch=1,
            grid=(4,),
            in_specs=[pl.BlockSpec((rows // 4, half), lambda i, c: (i, 1 - c[0]))],
            out_specs=pl.BlockSpec((rows // 4, half), lambda i, c: (i, 0)),
        ),
        out_shape=jax.ShapeDtypeStruct((rows, half), x.dtype),
        cost_estimate=pl.CostEstimate(
            flops=0, bytes_accessed=4 * rows * half, transcendentals=0
        ),
        name="half_of_query",
    )(core, x)


def spatial_kernel(level_ref, q_ref, k_ref, v_ref, gate_ref, o_ref):
    tokens = q_ref.shape[0]
    step = tokens // 3
    k = k_ref[...]
    v = v_ref[...]
    gate = gate_ref[0, 0:1, :]
    for at in range(0, tokens, step):
        scores = lax.dot_general(
            q_ref[at : at + step, :],
            k,
            (((1,), (1,)), ((), ())),
            preferred_element_type=jnp.float32,
        )
        scores = scores * SCALE
        expd = jnp.exp(scores - jnp.max(scores, axis=-1, keepdims=True))
        total = jnp.sum(expd, axis=-1, keepdims=True)
        weights = (expd * (1.0 / total)).astype(jnp.bfloat16)
        mixed = lax.dot_general(
            weights, v, (((1,), (0,)), ((), ())), preferred_element_type=jnp.float32
        )
        o_ref[at : at + step, :] = gate * mixed


def spatial(level, query, keys, values, gate_table, first):
    tokens = query.shape[0]
    col = pl.BlockSpec((tokens, HEAD_DIM), lambda h, lv: (0, first + h))
    return pl.pallas_call(
        spatial_kernel,
        grid_spec=pltpu.PrefetchScalarGridSpec(
            num_scalar_prefetch=1,
            grid=(HEADS_PER_CALL,),
            in_specs=[
                col,
                col,
                col,
                pl.BlockSpec((1, 2, HEAD_DIM), lambda h, lv: (lv[0], 0, first + h)),
            ],
            out_specs=pl.BlockSpec((tokens, HEAD_DIM), lambda h, lv: (0, h)),
        ),
        out_shape=jax.ShapeDtypeStruct((tokens, HEADS_PER_CALL * HEAD_DIM), jnp.float32),
        cost_estimate=pl.CostEstimate(
            flops=4 * HEADS_PER_CALL * tokens * tokens * HEAD_DIM,
            bytes_accessed=10 * tokens * HEADS_PER_CALL * HEAD_DIM,
            transcendentals=HEADS_PER_CALL * tokens * tokens,
        ),
        name="spatial",
    )(level, query, keys, values, gate_table)


def temporal_kernel(valid_ref, core_ref, qa_ref, qb_ref, *refs):
    frames = refs[:6]
    outs = refs[6:8]
    ones = jnp.ones((HEAD_DIM, HEAD_DIM), jnp.bfloat16)
    for at in range(0, qa_ref.shape[1], HEAD_DIM):
        span = slice(at, at + HEAD_DIM)
        near_keys = [f[0, :, span].astype(jnp.float32) for f in frames]
        for which, q_ref in enumerate((qa_ref, qb_ref)):
            q = q_ref[:, span].astype(jnp.float32) * SCALE
            scores = []
            for f in range(6):
                product = q * near_keys[f]
                high = product.astype(jnp.bfloat16)
                low = (product - high.astype(jnp.float32)).astype(jnp.bfloat16)
                score = jnp.dot(high, ones, preferred_element_type=jnp.float32)
                score = score + jnp.dot(low, ones, preferred_element_type=jnp.float32)
                scores.append(jnp.where(valid_ref[which * 6 + f] > 0, score, -1e30))
            top = functools.reduce(jnp.maximum, scores)
            expd = [jnp.exp(s - top) for s in scores]
            total = functools.reduce(jnp.add, expd)
            mixed = functools.reduce(
                jnp.add, [expd[f] * frames[f][1, :, span].astype(jnp.float32) for f in range(6)]
            )
            outs[which][:, span] = (mixed / total).astype(jnp.bfloat16)


def temporal(valid, core, query, query_b, frames, chunk, rows):
    half = query_b.shape[1]
    heads_here = half // HEAD_DIM
    step = 2
    width = step * HEAD_DIM
    grid = heads_here // step
    frame = pl.BlockSpec((2, rows, width), lambda i, va, c: (0, 0, i))
    out = pl.BlockSpec((rows, width), lambda i, va, c: (0, i))
    shape = jax.ShapeDtypeStruct((rows, half), jnp.bfloat16)
    return pl.pallas_call(
        temporal_kernel,
        grid_spec=pltpu.PrefetchScalarGridSpec(
            num_scalar_prefetch=2,
            grid=(grid,),
            in_specs=[
                pl.BlockSpec((rows, width), lambda i, va, c: (chunk, c[0] * grid + i)),
                pl.BlockSpec((rows, width), lambda i, va, c: (chunk, i)),
            ]
            + [frame] * 6,
            out_specs=[out, out],
        ),
        out_shape=[shape, shape],
        cost_estimate=pl.CostEstimate(
            flops=48 * rows * half, bytes_accessed=32 * rows * half, transcendentals=12 * rows * half
        ),
        name="temporal",
    )(valid, core, query, query_b, *frames)


def blend_kernel(core_ref, level_ref, gate_ref, mine_ref, other_ref, *refs):
    parts = refs[: HEADS // HEADS_PER_CALL]
    o_ref = refs[-1]
    core = core_ref[0]
    half = mine_ref.shape[1]
    width = HEADS_PER_CALL * HEAD_DIM
    grain = math.gcd(half, width)
    for at in range(0, 2 * half, grain):
        side = at // half
        inner = slice(at - side * half, at - side * half + grain)
        temporal_part = jnp.where(core == side, mine_ref[:, inner], other_ref[:, inner])
        start = at % width
        spatial_part = parts[at // width][:, start : start + grain]
        gate = gate_ref[0, 1:2, at : at + grain]
        o_ref[0, :, at : at + grain] = (
            spatial_part + gate * temporal_part.astype(jnp.float32)
        ).astype(o_ref.dtype)


def blend(core, level, gate_table, mine, other, parts, held, chunk, tokens):
    rows, half = mine.shape
    piece = pl.BlockSpec((rows, half), lambda i, c, lv: (0, 0))
    part = pl.BlockSpec((rows, HEADS_PER_CALL * HEAD_DIM), lambda i, c, lv: (chunk, 0))
    in_specs = [
        pl.BlockSpec((1, 2, 2 * half), lambda i, c, lv: (lv[0], 0, 0)),
        piece,
        piece,
    ] + [part] * len(parts)
    operands = [core, level, gate_table, mine, other] + list(parts)
    aliases = {}
    if held is not None:
        in_specs.append(pl.BlockSpec(memory_space=pl.ANY))
        aliases = {len(operands): 0}
        operands.append(held)
    return pl.pallas_call(
        blend_kernel,
        grid_spec=pltpu.PrefetchScalarGridSpec(
            num_scalar_prefetch=2,
            grid=(1,),
            in_specs=in_specs,
            out_specs=pl.BlockSpec((1, rows, 2 * half), lambda i, c, lv: (0, chunk, 0)),
        ),
        out_shape=jax.ShapeDtypeStruct((1, tokens, 2 * half), jnp.bfloat16),
        input_output_aliases=aliases,
        cost_estimate=pl.CostEstimate(
            flops=4 * rows * half, bytes_accessed=16 * rows * half, transcendentals=0
        ),
        name="blend",
    )(*operands)


def body(query, keys, values, gate_table, levels, window, queue_head):
    query, keys, values = query[0], keys[0], values[0]
    tokens = query.shape[0]
    rows = tokens // CHUNKS
    slot_count = lax.axis_size("queue")
    own = lax.axis_index("queue")
    core = (own & 1).astype(jnp.int32).reshape(1)

    slot_ids = jnp.arange(slot_count, dtype=jnp.int32)
    level = jnp.sum(jnp.where(slot_ids == own, levels, 0)).reshape(1)
    far = jnp.where(own & 2, own + 2, own - 2 + slot_count) % slot_count
    asking = jnp.stack([own, own ^ 1])
    given = jnp.stack([own, own ^ 1, own ^ 2, own ^ 3, far, far ^ 1])
    width = jnp.sum(jnp.where(slot_ids[None, :] == asking[:, None], window[None, :], 0), axis=1)
    position = (asking - queue_head[0]) % slot_count
    offset = (
        given[None, :] - asking[:, None] + slot_count + slot_count // 2
    ) % slot_count - slot_count // 2
    reached = position[:, None] + offset
    valid = (
        (jnp.abs(offset) <= jnp.minimum(width, REACH)[:, None])
        & (reached >= 0)
        & (reached < slot_count)
    )
    valid = valid.astype(jnp.int32).reshape(12)

    mine, theirs, first, first_b, second, second_b, results = [], [], [], [], [], [], []
    for chunk in range(CHUNKS):
        a, b = pack(core, keys, values, chunk, rows)
        mine.append(a)
        theirs.append(moved(b, "queue", other_core))
    query_b = moved(other_half(core, query), "queue", other_core)
    for chunk in range(CHUNKS):
        first.append(moved(mine[chunk], "queue", pair_chip))
        first_b.append(moved(theirs[chunk], "queue", pair_chip))
    for chunk in range(CHUNKS):
        second.append(moved(first[chunk], "queue", onward))
        second_b.append(moved(first_b[chunk], "queue", onward))
    parts = [
        spatial(level, query, keys, values, gate_table, h) for h in range(0, HEADS, HEADS_PER_CALL)
    ]
    result = None
    for chunk in range(CHUNKS):
        frames = [
            mine[chunk],
            theirs[chunk],
            first[chunk],
            first_b[chunk],
            second[chunk],
            second_b[chunk],
        ]
        kept, sent = temporal(valid, core, query, query_b, frames, chunk, rows)
        back = moved(sent, "queue", other_core)
        result = blend(core, level, gate_table, kept, back, parts, result, chunk, tokens)
    return result


def solution(mesh):
    in_specs = (
        P(("groups", "queue"), None, None),
        P(("groups", "queue"), None, None),
        P(("groups", "queue"), None, None),
        P(),
        P("groups"),
        P("groups"),
        P("groups"),
    )
    out_specs = P(("groups", "queue"), None, None)
    return jax.shard_map(body, mesh=mesh, in_specs=in_specs, out_specs=out_specs, check_vma=False)
```

```python
import functools
import math

import jax
import jax.numpy as jnp
from jax import lax
from jax.experimental import pallas as pl
from jax.experimental.pallas import tpu as pltpu
from jax.sharding import PartitionSpec as P


HEADS = 20
HEAD_DIM = 128
REACH = 2
ROWS = 96
HEADS_PER_CALL = 4
SPATIAL_ROWS = 384
SCALE = 1.0 / math.sqrt(HEAD_DIM)
LOG2_E = math.log2(math.e)


def moved(value, axis, where_to):
    count = lax.axis_size(axis)
    return lax.ppermute(value, axis, [(source, where_to(source) % count) for source in range(count)])


def other_core(index):
    return index ^ 1


def pair_chip(index):
    return index ^ 2


def onward(index):
    return index - 4 if index & 2 else index + 4


def pack_kernel(core_ref, k_mine, v_mine, k_other, v_other, mine_ref, other_ref):
    mine_ref[0] = k_mine[...]
    mine_ref[1] = v_mine[...]
    other_ref[0] = k_other[...]
    other_ref[1] = v_other[...]


def pack(core, keys, values, chunk, rows):
    half = keys.shape[1] // 2
    mine = pl.BlockSpec((rows, half), lambda i, c: (chunk, c[0]))
    other = pl.BlockSpec((rows, half), lambda i, c: (chunk, 1 - c[0]))
    whole = pl.BlockSpec((2, rows, half), lambda i, c: (0, 0, 0))
    shape = jax.ShapeDtypeStruct((2, rows, half), keys.dtype)
    return pl.pallas_call(
        pack_kernel,
        grid_spec=pltpu.PrefetchScalarGridSpec(
            num_scalar_prefetch=1,
            grid=(1,),
            in_specs=[mine, mine, other, other],
            out_specs=[whole, whole],
        ),
        out_shape=[shape, shape],
        cost_estimate=pl.CostEstimate(
            flops=0, bytes_accessed=16 * rows * half, transcendentals=0
        ),
        name="pack",
    )(core, keys, values, keys, values)


def half_kernel(core_ref, x_ref, o_ref):
    o_ref[...] = x_ref[...]


def other_half(core, x):
    rows, half = x.shape[0], x.shape[1] // 2
    return pl.pallas_call(
        half_kernel,
        grid_spec=pltpu.PrefetchScalarGridSpec(
            num_scalar_prefetch=1,
            grid=(4,),
            in_specs=[pl.BlockSpec((rows // 4, half), lambda i, c: (i, 1 - c[0]))],
            out_specs=pl.BlockSpec((rows // 4, half), lambda i, c: (i, 0)),
        ),
        out_shape=jax.ShapeDtypeStruct((rows, half), x.dtype),
        cost_estimate=pl.CostEstimate(
            flops=0, bytes_accessed=4 * rows * half, transcendentals=0
        ),
        name="half_of_query",
    )(core, x)


def spatial_kernel(level_ref, q_ref, k_ref, v_ref, gate_ref, o_ref):
    tokens = q_ref.shape[0]
    step = math.gcd(tokens, SPATIAL_ROWS)
    k = k_ref[...]
    v = v_ref[...]
    gate = gate_ref[0, 0:1, :]
    for at in range(0, tokens, step):
        scores = lax.dot_general(
            q_ref[at : at + step, :],
            k,
            (((1,), (1,)), ((), ())),
            preferred_element_type=jnp.float32,
        )
        expd = jnp.exp2((scores - jnp.max(scores, axis=-1, keepdims=True)) * (SCALE * LOG2_E))
        total = jnp.sum(expd, axis=-1, keepdims=True)
        mixed = lax.dot_general(
            expd.astype(jnp.bfloat16),
            v,
            (((1,), (0,)), ((), ())),
            preferred_element_type=jnp.float32,
        )
        o_ref[at : at + step, :] = mixed * (gate * (1.0 / total))


def spatial(level, query, keys, values, gate_table, first):
    tokens = query.shape[0]
    col = pl.BlockSpec((tokens, HEAD_DIM), lambda h, lv: (0, first + h))
    return pl.pallas_call(
        spatial_kernel,
        grid_spec=pltpu.PrefetchScalarGridSpec(
            num_scalar_prefetch=1,
            grid=(HEADS_PER_CALL,),
            in_specs=[
                col,
                col,
                col,
                pl.BlockSpec((1, 2, HEAD_DIM), lambda h, lv: (lv[0], 0, first + h)),
            ],
            out_specs=pl.BlockSpec((tokens, HEAD_DIM), lambda h, lv: (0, h)),
        ),
        out_shape=jax.ShapeDtypeStruct((tokens, HEADS_PER_CALL * HEAD_DIM), jnp.float32),
        cost_estimate=pl.CostEstimate(
            flops=4 * HEADS_PER_CALL * tokens * tokens * HEAD_DIM,
            bytes_accessed=10 * tokens * HEADS_PER_CALL * HEAD_DIM,
            transcendentals=HEADS_PER_CALL * tokens * tokens,
        ),
        name="spatial",
    )(level, query, keys, values, gate_table)


def temporal_kernel(valid_ref, core_ref, qa_ref, qb_ref, *refs):
    frames = refs[:6]
    outs = refs[6:8]
    rows, width = qa_ref.shape
    step = 16
    for at in range(0, width, HEAD_DIM):
        span = slice(at, at + HEAD_DIM)
        for low in range(0, rows, step):
            part = slice(low, low + step)
            near_keys = [f[0, part, span].astype(jnp.float32) for f in frames]
            for which, q_ref in enumerate((qa_ref, qb_ref)):
                q = q_ref[part, span].astype(jnp.float32) * (SCALE * LOG2_E)
                scores = []
                for f in range(6):
                    score = jnp.sum(q * near_keys[f], axis=-1, keepdims=True)
                    score = jnp.broadcast_to(score, q.shape)
                    scores.append(jnp.where(valid_ref[which * 6 + f] > 0, score, -1e30))
                top = functools.reduce(jnp.maximum, scores)
                expd = [jnp.exp2(s - top) for s in scores]
                total = functools.reduce(jnp.add, expd)
                mixed = functools.reduce(
                    jnp.add,
                    [expd[f] * frames[f][1, part, span].astype(jnp.float32) for f in range(6)],
                )
                outs[which][part, span] = (mixed * (1.0 / total)).astype(jnp.bfloat16)


def temporal(valid, core, query, query_b, frames, chunk, rows):
    half = query_b.shape[1]
    heads_here = half // HEAD_DIM
    step = 2
    width = step * HEAD_DIM
    grid = heads_here // step
    frame = pl.BlockSpec((2, rows, width), lambda i, va, c: (0, 0, i))
    out = pl.BlockSpec((rows, width), lambda i, va, c: (0, i))
    shape = jax.ShapeDtypeStruct((rows, half), jnp.bfloat16)
    return pl.pallas_call(
        temporal_kernel,
        grid_spec=pltpu.PrefetchScalarGridSpec(
            num_scalar_prefetch=2,
            grid=(grid,),
            in_specs=[
                pl.BlockSpec((rows, width), lambda i, va, c: (chunk, c[0] * grid + i)),
                pl.BlockSpec((rows, width), lambda i, va, c: (chunk, i)),
            ]
            + [frame] * 6,
            out_specs=[out, out],
        ),
        out_shape=[shape, shape],
        cost_estimate=pl.CostEstimate(
            flops=48 * rows * half, bytes_accessed=32 * rows * half, transcendentals=12 * rows * half
        ),
        name="temporal",
    )(valid, core, query, query_b, *frames)


def blend_kernel(core_ref, level_ref, gate_ref, mine_ref, other_ref, *refs):
    parts = refs[: HEADS // HEADS_PER_CALL]
    o_ref = refs[-1]
    core = core_ref[0]
    half = mine_ref.shape[1]
    width = HEADS_PER_CALL * HEAD_DIM
    grain = math.gcd(half, width)
    for at in range(0, 2 * half, grain):
        side = at // half
        inner = slice(at - side * half, at - side * half + grain)
        temporal_part = jnp.where(core == side, mine_ref[:, inner], other_ref[:, inner])
        start = at % width
        spatial_part = parts[at // width][:, start : start + grain]
        gate = gate_ref[0, 1:2, at : at + grain]
        o_ref[0, :, at : at + grain] = (
            spatial_part + gate * temporal_part.astype(jnp.float32)
        ).astype(o_ref.dtype)


def blend(core, level, gate_table, mine, other, parts, held, chunk, tokens):
    rows, half = mine.shape
    piece = pl.BlockSpec((rows, half), lambda i, c, lv: (0, 0))
    part = pl.BlockSpec((rows, HEADS_PER_CALL * HEAD_DIM), lambda i, c, lv: (chunk, 0))
    in_specs = [
        pl.BlockSpec((1, 2, 2 * half), lambda i, c, lv: (lv[0], 0, 0)),
        piece,
        piece,
    ] + [part] * len(parts)
    operands = [core, level, gate_table, mine, other] + list(parts)
    aliases = {}
    if held is not None:
        in_specs.append(pl.BlockSpec(memory_space=pl.ANY))
        aliases = {len(operands): 0}
        operands.append(held)
    return pl.pallas_call(
        blend_kernel,
        grid_spec=pltpu.PrefetchScalarGridSpec(
            num_scalar_prefetch=2,
            grid=(1,),
            in_specs=in_specs,
            out_specs=pl.BlockSpec((1, rows, 2 * half), lambda i, c, lv: (0, chunk, 0)),
        ),
        out_shape=jax.ShapeDtypeStruct((1, tokens, 2 * half), jnp.bfloat16),
        input_output_aliases=aliases,
        cost_estimate=pl.CostEstimate(
            flops=4 * rows * half, bytes_accessed=16 * rows * half, transcendentals=0
        ),
        name="blend",
    )(*operands)


def body(query, keys, values, gate_table, levels, window, queue_head):
    query, keys, values = query[0], keys[0], values[0]
    tokens = query.shape[0]
    rows = ROWS
    slot_count = lax.axis_size("queue")
    own = lax.axis_index("queue")
    core = (own & 1).astype(jnp.int32).reshape(1)

    slot_ids = jnp.arange(slot_count, dtype=jnp.int32)
    level = jnp.sum(jnp.where(slot_ids == own, levels, 0)).reshape(1)
    far = jnp.where(own & 2, own + 2, own - 2 + slot_count) % slot_count
    asking = jnp.stack([own, own ^ 1])
    given = jnp.stack([own, own ^ 1, own ^ 2, own ^ 3, far, far ^ 1])
    width = jnp.sum(jnp.where(slot_ids[None, :] == asking[:, None], window[None, :], 0), axis=1)
    position = (asking - queue_head[0]) % slot_count
    offset = (
        given[None, :] - asking[:, None] + slot_count + slot_count // 2
    ) % slot_count - slot_count // 2
    reached = position[:, None] + offset
    valid = (
        (jnp.abs(offset) <= jnp.minimum(width, REACH)[:, None])
        & (reached >= 0)
        & (reached < slot_count)
    )
    valid = valid.astype(jnp.int32).reshape(12)

    chunks = tokens // rows
    value = {}
    held = {None: None}

    def permute(name, source, where_to):
        value[name] = moved(value[source], "queue", where_to)

    def emit(name):
        kind, at = name[:2], int(name[2:] or 0)
        if kind == "pk":
            value[f"A{at}"], value[f"O{at}"] = pack(core, keys, values, at, rows)
        elif kind == "hq":
            value["HQ"] = other_half(core, query)
        elif kind == "qx":
            permute("QB", "HQ", other_core)
        elif kind == "th":
            permute(f"B{at}", f"O{at}", other_core)
        elif kind in ("fa", "fb"):
            permute(f"1{kind[1]}{at}", f"{kind[1].upper()}{at}", pair_chip)
        elif kind in ("sa", "sb"):
            permute(f"2{kind[1]}{at}", f"1{kind[1]}{at}", onward)
        elif kind == "sp":
            value[name] = spatial(level, query, keys, values, gate_table, at * HEADS_PER_CALL)
        elif kind == "te":
            frames = [value[f"{n}{at}"] for n in ("A", "B", "1a", "1b", "2a", "2b")]
            value[f"K{at}"], value[f"S{at}"] = temporal(
                valid, core, query, value["QB"], frames, at, rows
            )
        elif kind == "re":
            permute(f"R{at}", f"S{at}", other_core)
        elif kind == "bl":
            parts = [value[f"sp{h}"] for h in range(HEADS // HEADS_PER_CALL)]
            held[None] = blend(
                core, level, gate_table, value[f"K{at}"], value[f"R{at}"], parts,
                held[None], at, tokens,
            )

    for name in plan(chunks):
        emit(name)
    return held[None]


def plan(chunks):
    order = ["pk0", "th0", "fa0", "pk1", "th1", "fb0", "fa1", "hq", "qx"]
    spatials = [f"sp{h}" for h in range(HEADS // HEADS_PER_CALL)]
    stage_one = [f"f{c}{j}" for j in range(chunks) for c in "ab"][3:]
    packs = [(f"pk{j}", f"th{j}") for j in range(2, chunks)]
    order.append(spatials.pop(0))
    for grain in range(2 * chunks):
        order.append(f"s{'ab'[grain % 2]}{grain // 2}")
        if stage_one:
            order.append(stage_one.pop(0))
        if grain % 2 == 0 and packs:
            order.extend(packs.pop(0))
        if grain % 2 == 1 and grain >= 3:
            pair = (grain - 3) // 2
            order += [f"te{pair}", f"re{pair}"]
            if pair >= 3:
                order.append(f"bl{pair - 3}")
        elif spatials:
            order.append(spatials.pop(0))
    order += spatials
    order += [f"bl{j}" for j in range(chunks - 4, chunks - 1)]
    order += [f"te{chunks - 1}", f"re{chunks - 1}", f"bl{chunks - 1}"]
    return order


def solution(mesh):
    in_specs = (
        P(("groups", "queue"), None, None),
        P(("groups", "queue"), None, None),
        P(("groups", "queue"), None, None),
        P(),
        P("groups"),
        P("groups"),
        P("groups"),
    )
    out_specs = P(("groups", "queue"), None, None)

    return jax.shard_map(body, mesh=mesh, in_specs=in_specs, out_specs=out_specs, check_vma=False)
```

```python
import functools
import math

import jax
import jax.numpy as jnp
from jax import lax
from jax.experimental import pallas as pl
from jax.experimental.pallas import tpu as pltpu
from jax.sharding import PartitionSpec as P


HEAD_DIM = 128
REACH = 2
CALL_VMEM = 16 << 20
SCALE = 1.0 / math.sqrt(HEAD_DIM)
LOG2_E = math.log2(math.e)
SPATIAL_ROWS = 384
CHUNKS = [(720, 48)] + [(80 * i, 80) for i in range(8)] + [(672, 48), (640, 32)]
HEAD_RUNS = [4, 4, 4, 4, 4]


def moved(value, axis, where_to):
    count = lax.axis_size(axis)
    return lax.ppermute(value, axis, [(source, where_to(source) % count) for source in range(count)])


def other_core(index):
    return index ^ 1


def pair_chip(index):
    return index ^ 2


def pair_chip_other_core(index):
    return index ^ 3


def onward(index):
    return index - 4 if index & 2 else index + 4


def pack_kernel(chunks, core_ref, k_ref, v_ref, *refs):
    count = len(chunks)
    outs, held, read_sem, write_sem = refs[: 2 * count], refs[-3], refs[-2], refs[-1]
    half = k_ref.shape[1] // 2
    core = core_ref[0]

    def reads(i, side):
        low, rows = chunks[i]
        at = sum(n for _, n in chunks[:i])
        from_column = pl.multiple_of((core if side == 0 else 1 - core) * half, half)
        return [
            pltpu.make_async_copy(
                source.at[pl.ds(low, rows), pl.ds(from_column, half)],
                held.at[side, plane, pl.ds(at, rows), :],
                read_sem.at[2 * i + side, plane],
            )
            for plane, source in enumerate((k_ref, v_ref))
        ]

    def write(i, side):
        rows = chunks[i][1]
        at = sum(n for _, n in chunks[:i])
        return pltpu.make_async_copy(
            held.at[side, :, pl.ds(at, rows), :], outs[2 * i + side], write_sem.at[2 * i + side]
        )

    pieces = [(i, side) for i in range(count) for side in range(2)]
    for piece in pieces:
        for copy in reads(*piece):
            copy.start()
    for piece in pieces:
        for copy in reads(*piece):
            copy.wait()
        write(*piece).start()
    for piece in pieces:
        write(*piece).wait()


def pack(core, keys, values, chunks):
    half = keys.shape[1] // 2
    total = sum(rows for _, rows in chunks)
    anywhere = pl.BlockSpec(memory_space=pl.ANY)
    return pl.pallas_call(
        functools.partial(pack_kernel, chunks),
        grid_spec=pltpu.PrefetchScalarGridSpec(
            num_scalar_prefetch=1,
            grid=(1,),
            in_specs=[anywhere, anywhere],
            out_specs=[anywhere] * (2 * len(chunks)),
            scratch_shapes=[
                pltpu.VMEM((2, 2, total, half), keys.dtype),
                pltpu.SemaphoreType.DMA((2 * len(chunks), 2)),
                pltpu.SemaphoreType.DMA((2 * len(chunks),)),
            ],
        ),
        out_shape=[
            jax.ShapeDtypeStruct((2, rows, half), keys.dtype) for _, rows in chunks for _ in range(2)
        ],
        cost_estimate=pl.CostEstimate(
            flops=0, bytes_accessed=16 * total * half, transcendentals=0
        ),
        name="pack",
    )(core, keys, values)


def spatial_kernel(level_ref, q_ref, k_ref, v_ref, gate_ref, *refs):
    o_ref = refs[-1]
    tokens = q_ref.shape[0]
    step = math.gcd(tokens, SPATIAL_ROWS)
    k = k_ref[...]
    v = v_ref[...]
    gate = gate_ref[0, 0:1, :]
    for at in range(0, tokens, step):
        scores = lax.dot_general(
            q_ref[at : at + step, :],
            k,
            (((1,), (1,)), ((), ())),
            preferred_element_type=jnp.float32,
        )
        expd = jnp.exp2((scores - jnp.max(scores, axis=-1, keepdims=True)) * (SCALE * LOG2_E))
        total = jnp.sum(expd, axis=-1, keepdims=True)
        mixed = lax.dot_general(
            expd.astype(jnp.bfloat16),
            v,
            (((1,), (0,)), ((), ())),
            preferred_element_type=jnp.float32,
        )
        o_ref[at : at + step, :] = mixed * (gate * (1.0 / total))


def spatial(level, query, keys, values, gate_table, first, heads, held):
    tokens, width = query.shape
    col = pl.BlockSpec((tokens, HEAD_DIM), lambda h, lv: (0, first + h))
    in_specs = [
        col,
        col,
        col,
        pl.BlockSpec((1, 2, HEAD_DIM), lambda h, lv: (lv[0], 0, first + h)),
    ]
    operands = [level, query, keys, values, gate_table]
    aliases = {}
    if held is not None:
        in_specs.append(pl.BlockSpec(memory_space=pl.ANY))
        aliases = {len(operands): 0}
        operands.append(held)
    return pl.pallas_call(
        spatial_kernel,
        grid_spec=pltpu.PrefetchScalarGridSpec(
            num_scalar_prefetch=1,
            grid=(heads,),
            in_specs=in_specs,
            out_specs=col,
        ),
        out_shape=jax.ShapeDtypeStruct((tokens, width), jnp.float32),
        input_output_aliases=aliases,
        cost_estimate=pl.CostEstimate(
            flops=4 * heads * tokens * tokens * HEAD_DIM,
            bytes_accessed=10 * tokens * heads * HEAD_DIM,
            transcendentals=heads * tokens * tokens,
        ),
        compiler_params=pltpu.CompilerParams(vmem_limit_bytes=CALL_VMEM),
        name="spatial",
    )(*operands)


def temporal_kernel(valid_ref, core_ref, qa_ref, ka_ref, va_ref, qb_ref, kb_ref, vb_ref, *refs):
    frames, outs = refs[:4], refs[4:6]
    rows, width = qa_ref.shape
    step = 16
    for at in range(0, width, HEAD_DIM):
        span = slice(at, at + HEAD_DIM)
        for low in range(0, rows, step):
            part = slice(low, low + step)
            near_keys = [r[part, span] for r in (ka_ref, kb_ref)]
            near_keys += [f[0, part, span] for f in frames]
            near_values = [r[part, span] for r in (va_ref, vb_ref)]
            near_values += [f[1, part, span] for f in frames]
            near_keys = [x.astype(jnp.float32) for x in near_keys]
            for which, q_ref in enumerate((qa_ref, qb_ref)):
                q = q_ref[part, span].astype(jnp.float32) * (SCALE * LOG2_E)
                scores = []
                for f in range(6):
                    score = jnp.sum(q * near_keys[f], axis=-1, keepdims=True)
                    score = jnp.broadcast_to(score, q.shape)
                    scores.append(jnp.where(valid_ref[which * 6 + f] > 0, score, -1e30))
                top = functools.reduce(jnp.maximum, scores)
                expd = [jnp.exp2(s - top) for s in scores]
                total = functools.reduce(jnp.add, expd)
                mixed = functools.reduce(
                    jnp.add, [expd[f] * near_values[f].astype(jnp.float32) for f in range(6)]
                )
                outs[which][part, span] = (mixed * (1.0 / total)).astype(jnp.bfloat16)


def temporal(valid, core, own, partner, frames, chunk):
    low, rows = chunk
    half = own[0].shape[1] // 2
    steps = 2 if rows > 32 else 1
    width = half // steps
    at = low // rows
    mine = pl.BlockSpec((rows, width), lambda i, va, c: (at, steps * c[0] + i))
    frame = pl.BlockSpec((2, rows, width), lambda i, va, c: (0, 0, i))
    out = pl.BlockSpec((rows, width), lambda i, va, c: (0, i))
    shape = jax.ShapeDtypeStruct((rows, half), jnp.bfloat16)
    return pl.pallas_call(
        temporal_kernel,
        grid_spec=pltpu.PrefetchScalarGridSpec(
            num_scalar_prefetch=2,
            grid=(steps,),
            in_specs=[mine] * 6 + [frame] * 4,
            out_specs=[out, out],
        ),
        out_shape=[shape, shape],
        cost_estimate=pl.CostEstimate(
            flops=72 * rows * half, bytes_accessed=32 * rows * half, transcendentals=12 * rows * half
        ),
        compiler_params=pltpu.CompilerParams(vmem_limit_bytes=CALL_VMEM),
        name="temporal",
    )(valid, core, *own, *partner, *frames)


def blend_kernel(count, core_ref, level_ref, gate_ref, part_ref, *refs):
    o_ref = refs[-1]
    core = core_ref[0]
    half = part_ref.shape[1] // 2

    def piece(mine_ref, other_ref):
        for side in range(2):
            span = slice(side * half, (side + 1) * half)
            temporal_part = jnp.where(core == side, mine_ref[...], other_ref[...])
            o_ref[0, :, span] = (
                part_ref[:, span] + gate_ref[0, 1:2, span] * temporal_part.astype(jnp.float32)
            ).astype(o_ref.dtype)

    if count == 1:
        piece(refs[0], refs[1])
    else:
        for i in range(count):
            pl.when(pl.program_id(0) == i)(functools.partial(piece, refs[2 * i], refs[2 * i + 1]))


def blend(core, level, gate_table, halves, part, held, chunks):
    tokens, width = part.shape
    low, rows = chunks[0]
    at = low // rows
    count = len(chunks)
    piece = pl.BlockSpec((rows, width // 2), lambda i, c, lv: (0, 0))
    in_specs = [
        pl.BlockSpec((1, 2, width), lambda i, c, lv: (lv[0], 0, 0)),
        pl.BlockSpec((rows, width), lambda i, c, lv: (at + i, 0)),
    ] + [piece] * (2 * count)
    operands = [core, level, gate_table, part] + list(halves)
    aliases = {}
    if held is not None:
        in_specs.append(pl.BlockSpec(memory_space=pl.ANY))
        aliases = {len(operands): 0}
        operands.append(held)
    return pl.pallas_call(
        functools.partial(blend_kernel, count),
        grid_spec=pltpu.PrefetchScalarGridSpec(
            num_scalar_prefetch=2,
            grid=(count,),
            in_specs=in_specs,
            out_specs=pl.BlockSpec((1, rows, width), lambda i, c, lv: (0, at + i, 0)),
        ),
        out_shape=jax.ShapeDtypeStruct((1, tokens, width), jnp.bfloat16),
        input_output_aliases=aliases,
        cost_estimate=pl.CostEstimate(
            flops=2 * count * rows * width,
            bytes_accessed=8 * count * rows * width,
            transcendentals=0,
        ),
        compiler_params=pltpu.CompilerParams(vmem_limit_bytes=CALL_VMEM),
        name="blend",
    )(*operands)


def body(query, keys, values, gate_table, levels, window, queue_head):
    query, keys, values = (
        pltpu.with_memory_space_constraint(x[0], pltpu.HBM) for x in (query, keys, values)
    )
    slot_count = lax.axis_size("queue")
    own = lax.axis_index("queue")
    core = (own & 1).astype(jnp.int32).reshape(1)

    slot_ids = jnp.arange(slot_count, dtype=jnp.int32)
    level = jnp.sum(jnp.where(slot_ids == own, levels, 0)).reshape(1)
    far = jnp.where(own & 2, own + 2, own - 2 + slot_count) % slot_count
    asking = jnp.stack([own, own ^ 1])
    given = jnp.stack([own, own ^ 1, own ^ 2, own ^ 3, far, far ^ 1])
    width = jnp.sum(jnp.where(slot_ids[None, :] == asking[:, None], window[None, :], 0), axis=1)
    position = (asking - queue_head[0]) % slot_count
    offset = (
        given[None, :] - asking[:, None] + slot_count + slot_count // 2
    ) % slot_count - slot_count // 2
    reached = position[:, None] + offset
    valid = (
        (jnp.abs(offset) <= jnp.minimum(width, REACH)[:, None])
        & (reached >= 0)
        & (reached < slot_count)
    )
    valid = valid.astype(jnp.int32).reshape(12)

    value = {"k": keys, "v": values, "q": query}
    held = {"spatial": None, "result": None}

    def permute(name, source, where_to):
        value[name] = moved(value[source], "queue", where_to)

    def packed(indices):
        outs = pack(core, keys, values, [CHUNKS[i] for i in indices])
        for n, i in enumerate(indices):
            value[f"A{i}"], value[f"X{i}"] = outs[2 * n], outs[2 * n + 1]

    def emit(name):
        kind = name[:2]
        at = int(name[2:].split("_")[0] or 0)
        if kind == "pk":
            first, last = (int(n) for n in name[2:].split("_"))
            packed(range(first, last))
        elif kind in ("ek", "ev", "eq"):
            permute(kind, kind[1], other_core)
        elif kind == "fa":
            permute(f"1a{at}", f"A{at}", pair_chip)
        elif kind == "fx":
            permute(f"1x{at}", f"X{at}", pair_chip_other_core)
        elif kind in ("sa", "sx"):
            permute(f"2{kind[1]}{at}", f"1{kind[1]}{at}", onward)
        elif kind == "sp":
            held["spatial"] = spatial(
                level, query, keys, values, gate_table,
                sum(HEAD_RUNS[:at]), HEAD_RUNS[at], held["spatial"],
            )
        elif kind == "te":
            frames = [value[f"{n}{at}"] for n in ("1a", "1x", "2a", "2x")]
            value[f"K{at}"], value[f"S{at}"] = temporal(
                valid, core, (query, keys, values), (value["eq"], value["ek"], value["ev"]),
                frames, CHUNKS[at],
            )
        elif kind == "re":
            permute(f"R{at}", f"S{at}", other_core)
        elif kind == "bl":
            first, last = (int(n) for n in name[2:].split("_"))
            halves = [value[f"{n}{i}"] for i in range(first, last) for n in "KR"]
            held["result"] = blend(
                core, level, gate_table, halves, held["spatial"], held["result"],
                CHUNKS[first:last],
            )

    for name in PLAN:
        emit(name)
    return held["result"]


PLAN = [
    *("pk0_2", "fa0", "fx0", "fa1", "ek", "ev", "eq", "pk2_11"),
    *("sa0", "fx1", "fa2", "fx2"),
    *("sx0", "fa3", "fx3", "fa4", "fx4"),
    *("sa1", "fa5", "fx5", "fa6", "fx6"),
    *("sx1", "fa7", "fx7", "fa8", "fx8"),
    *("sa2", "fa9", "fx9", "fa10", "fx10"),
    *("sx2", "te0", "re0", "sa3", "sp0"),
    *("sx3", "te1", "re1", "sa4", "sp1"),
    *("sx4", "te2", "re2", "sa5", "sp2"),
    *("sx5", "te3", "re3", "sa6", "sp3"),
    *("sx6", "te4", "re4", "sa7", "sp4"),
    *("sx7", "te5", "re5", "sa8", "bl0_1", "bl1_5"),
    *("sx8", "te6", "re6", "sa9", "te7", "re7"),
    *("sx9", "te8", "re8", "sa10", "sx10", "bl5_8"),
    *("te9", "re9", "bl8_9", "bl9_10", "te10", "re10", "bl10_11"),
]


def solution(mesh):
    in_specs = (
        P(("groups", "queue"), None, None),
        P(("groups", "queue"), None, None),
        P(("groups", "queue"), None, None),
        P(),
        P("groups"),
        P("groups"),
        P("groups"),
    )
    out_specs = P(("groups", "queue"), None, None)

    return jax.shard_map(body, mesh=mesh, in_specs=in_specs, out_specs=out_specs, check_vma=False)
```

```python
import functools
import math

import jax
import jax.numpy as jnp
from jax import lax
from jax.experimental import pallas as pl
from jax.experimental.pallas import tpu as pltpu
from jax.sharding import PartitionSpec as P


HEAD_DIM = 128
REACH = 2
CALL_VMEM = 16 << 20
SCALE = 1.0 / math.sqrt(HEAD_DIM)
LOG2_E = math.log2(math.e)
SPATIAL_ROWS = 384
CHUNKS = [(640, 64)] + [(64 * i, 64) for i in range(10)] + [(704, 32), (736, 32)]
GROUPS = [[0], [1, 2], [3, 4], [5, 6], [7, 8], [9, 10], [11], [12]]
HEAD_RUNS = [2] * 10


def moved(value, axis, where_to):
    count = lax.axis_size(axis)
    return lax.ppermute(value, axis, [(source, where_to(source) % count) for source in range(count)])


def other_core(index):
    return index ^ 1


def pair_chip(index):
    return index ^ 2


def pair_chip_other_core(index):
    return index ^ 3


def onward(index):
    return index - 4 if index & 2 else index + 4


def pack_kernel(chunks, core_ref, k_ref, v_ref, *refs):
    count = len(chunks)
    outs, held, read_sem, write_sem = refs[: 2 * count], refs[-3], refs[-2], refs[-1]
    half = k_ref.shape[1] // 2
    core = core_ref[0]

    def reads(i, side):
        low, rows = chunks[i]
        at = sum(n for _, n in chunks[:i])
        from_column = pl.multiple_of((core if side == 0 else 1 - core) * half, half)
        return [
            pltpu.make_async_copy(
                source.at[pl.ds(low, rows), pl.ds(from_column, half)],
                held.at[side, plane, pl.ds(at, rows), :],
                read_sem.at[2 * i + side, plane],
            )
            for plane, source in enumerate((k_ref, v_ref))
        ]

    def write(i, side):
        rows = chunks[i][1]
        at = sum(n for _, n in chunks[:i])
        return pltpu.make_async_copy(
            held.at[side, :, pl.ds(at, rows), :], outs[2 * i + side], write_sem.at[2 * i + side]
        )

    pieces = [(i, side) for i in range(count) for side in range(2)]
    for piece in pieces:
        for copy in reads(*piece):
            copy.start()
    for piece in pieces:
        for copy in reads(*piece):
            copy.wait()
        write(*piece).start()
    for piece in pieces:
        write(*piece).wait()


def pack(core, keys, values, chunks):
    half = keys.shape[1] // 2
    total = sum(rows for _, rows in chunks)
    anywhere = pl.BlockSpec(memory_space=pl.ANY)
    return pl.pallas_call(
        functools.partial(pack_kernel, chunks),
        grid_spec=pltpu.PrefetchScalarGridSpec(
            num_scalar_prefetch=1,
            grid=(1,),
            in_specs=[anywhere, anywhere],
            out_specs=[anywhere] * (2 * len(chunks)),
            scratch_shapes=[
                pltpu.VMEM((2, 2, total, half), keys.dtype),
                pltpu.SemaphoreType.DMA((2 * len(chunks), 2)),
                pltpu.SemaphoreType.DMA((2 * len(chunks),)),
            ],
        ),
        out_shape=[
            jax.ShapeDtypeStruct((2, rows, half), keys.dtype) for _, rows in chunks for _ in range(2)
        ],
        cost_estimate=pl.CostEstimate(
            flops=0, bytes_accessed=16 * total * half, transcendentals=0
        ),
        name="pack",
    )(core, keys, values)


def spatial_kernel(level_ref, q_ref, k_ref, v_ref, gate_ref, *refs):
    o_ref = refs[-1]
    tokens = q_ref.shape[0]
    step = math.gcd(tokens, SPATIAL_ROWS)
    k = k_ref[...]
    v = v_ref[...]
    gate = gate_ref[0, 0:1, :]
    for at in range(0, tokens, step):
        scores = lax.dot_general(
            q_ref[at : at + step, :],
            k,
            (((1,), (1,)), ((), ())),
            preferred_element_type=jnp.float32,
        )
        expd = jnp.exp2((scores - jnp.max(scores, axis=-1, keepdims=True)) * (SCALE * LOG2_E))
        total = jnp.sum(expd, axis=-1, keepdims=True)
        mixed = lax.dot_general(
            expd.astype(jnp.bfloat16),
            v,
            (((1,), (0,)), ((), ())),
            preferred_element_type=jnp.float32,
        )
        o_ref[at : at + step, :] = mixed * (gate * (1.0 / total))


def spatial(level, query, keys, values, gate_table, first, heads, held):
    tokens, width = query.shape
    col = pl.BlockSpec((tokens, HEAD_DIM), lambda h, lv: (0, first + h))
    in_specs = [
        col,
        col,
        col,
        pl.BlockSpec((1, 2, HEAD_DIM), lambda h, lv: (lv[0], 0, first + h)),
    ]
    operands = [level, query, keys, values, gate_table]
    aliases = {}
    if held is not None:
        in_specs.append(pl.BlockSpec(memory_space=pl.ANY))
        aliases = {len(operands): 0}
        operands.append(held)
    return pl.pallas_call(
        spatial_kernel,
        grid_spec=pltpu.PrefetchScalarGridSpec(
            num_scalar_prefetch=1,
            grid=(heads,),
            in_specs=in_specs,
            out_specs=col,
        ),
        out_shape=jax.ShapeDtypeStruct((tokens, width), jnp.float32),
        input_output_aliases=aliases,
        cost_estimate=pl.CostEstimate(
            flops=4 * heads * tokens * tokens * HEAD_DIM,
            bytes_accessed=10 * tokens * heads * HEAD_DIM,
            transcendentals=heads * tokens * tokens,
        ),
        compiler_params=pltpu.CompilerParams(vmem_limit_bytes=CALL_VMEM),
        name="spatial",
    )(*operands)


def temporal_kernel(sizes, valid_ref, core_ref, *refs):
    qa_ref, ka_ref, va_ref, qb_ref, kb_ref, vb_ref = refs[:6]
    outs = refs[-2:]
    width = qa_ref.shape[1]
    step = 16
    for at in range(0, width, HEAD_DIM):
        span = slice(at, at + HEAD_DIM)
        start = 0
        for piece, rows in enumerate(sizes):
            frames = refs[6 + 4 * piece : 10 + 4 * piece]
            for low in range(0, rows, step):
                inner = slice(low, low + step)
                part = slice(start + low, start + low + step)
                near_keys = [r[part, span] for r in (ka_ref, kb_ref)]
                near_keys += [f[0, inner, span] for f in frames]
                near_values = [r[part, span] for r in (va_ref, vb_ref)]
                near_values += [f[1, inner, span] for f in frames]
                near_keys = [x.astype(jnp.float32) for x in near_keys]
                for which, q_ref in enumerate((qa_ref, qb_ref)):
                    q = q_ref[part, span].astype(jnp.float32) * (SCALE * LOG2_E)
                    scores = []
                    for f in range(6):
                        score = jnp.sum(q * near_keys[f], axis=-1, keepdims=True)
                        score = jnp.broadcast_to(score, q.shape)
                        scores.append(jnp.where(valid_ref[which * 6 + f] > 0, score, -1e30))
                    top = functools.reduce(jnp.maximum, scores)
                    expd = [jnp.exp2(s - top) for s in scores]
                    total = functools.reduce(jnp.add, expd)
                    mixed = functools.reduce(
                        jnp.add, [expd[f] * near_values[f].astype(jnp.float32) for f in range(6)]
                    )
                    outs[which][part, span] = (mixed * (1.0 / total)).astype(jnp.bfloat16)
            start += rows


def temporal(valid, core, own, partner, frames, chunks):
    low = chunks[0][0]
    sizes = [n for _, n in chunks]
    rows = sum(sizes)
    half = own[0].shape[1] // 2
    steps = 2 if rows > 32 else 1
    width = half // steps
    at = low // rows
    mine = pl.BlockSpec((rows, width), lambda i, va, c: (at, steps * c[0] + i))
    frame_specs = [pl.BlockSpec((2, n, width), lambda i, va, c: (0, 0, i)) for n in sizes]
    out = pl.BlockSpec((rows, width), lambda i, va, c: (0, i))
    shape = jax.ShapeDtypeStruct((rows, half), jnp.bfloat16)
    return pl.pallas_call(
        functools.partial(temporal_kernel, sizes),
        grid_spec=pltpu.PrefetchScalarGridSpec(
            num_scalar_prefetch=2,
            grid=(steps,),
            in_specs=[mine] * 6 + [spec for spec in frame_specs for _ in range(4)],
            out_specs=[out, out],
        ),
        out_shape=[shape, shape],
        cost_estimate=pl.CostEstimate(
            flops=72 * rows * half, bytes_accessed=32 * rows * half, transcendentals=12 * rows * half
        ),
        compiler_params=pltpu.CompilerParams(vmem_limit_bytes=CALL_VMEM),
        name="temporal",
    )(valid, core, *own, *partner, *frames)


def blend_kernel(count, core_ref, level_ref, gate_ref, part_ref, *refs):
    o_ref = refs[-1]
    core = core_ref[0]
    half = part_ref.shape[1] // 2

    def piece(mine_ref, other_ref):
        for side in range(2):
            span = slice(side * half, (side + 1) * half)
            temporal_part = jnp.where(core == side, mine_ref[...], other_ref[...])
            o_ref[0, :, span] = (
                part_ref[:, span] + gate_ref[0, 1:2, span] * temporal_part.astype(jnp.float32)
            ).astype(o_ref.dtype)

    if count == 1:
        piece(refs[0], refs[1])
    else:
        for i in range(count):
            pl.when(pl.program_id(0) == i)(functools.partial(piece, refs[2 * i], refs[2 * i + 1]))


def blend(core, level, gate_table, halves, part, held, chunks):
    tokens, width = part.shape
    low, rows = chunks[0]
    at = low // rows
    count = len(chunks)
    piece = pl.BlockSpec((rows, width // 2), lambda i, c, lv: (0, 0))
    in_specs = [
        pl.BlockSpec((1, 2, width), lambda i, c, lv: (lv[0], 0, 0)),
        pl.BlockSpec((rows, width), lambda i, c, lv: (at + i, 0)),
    ] + [piece] * (2 * count)
    operands = [core, level, gate_table, part] + list(halves)
    aliases = {}
    if held is not None:
        in_specs.append(pl.BlockSpec(memory_space=pl.ANY))
        aliases = {len(operands): 0}
        operands.append(held)
    return pl.pallas_call(
        functools.partial(blend_kernel, count),
        grid_spec=pltpu.PrefetchScalarGridSpec(
            num_scalar_prefetch=2,
            grid=(count,),
            in_specs=in_specs,
            out_specs=pl.BlockSpec((1, rows, width), lambda i, c, lv: (0, at + i, 0)),
        ),
        out_shape=jax.ShapeDtypeStruct((1, tokens, width), jnp.bfloat16),
        input_output_aliases=aliases,
        cost_estimate=pl.CostEstimate(
            flops=2 * count * rows * width,
            bytes_accessed=8 * count * rows * width,
            transcendentals=0,
        ),
        compiler_params=pltpu.CompilerParams(vmem_limit_bytes=CALL_VMEM),
        name="blend",
    )(*operands)


def body(query, keys, values, gate_table, levels, window, queue_head):
    query, keys, values = (
        pltpu.with_memory_space_constraint(x[0], pltpu.HBM) for x in (query, keys, values)
    )
    slot_count = lax.axis_size("queue")
    own = lax.axis_index("queue")
    core = (own & 1).astype(jnp.int32).reshape(1)

    slot_ids = jnp.arange(slot_count, dtype=jnp.int32)
    level = jnp.sum(jnp.where(slot_ids == own, levels, 0)).reshape(1)
    far = jnp.where(own & 2, own + 2, own - 2 + slot_count) % slot_count
    asking = jnp.stack([own, own ^ 1])
    given = jnp.stack([own, own ^ 1, own ^ 2, own ^ 3, far, far ^ 1])
    width = jnp.sum(jnp.where(slot_ids[None, :] == asking[:, None], window[None, :], 0), axis=1)
    position = (asking - queue_head[0]) % slot_count
    offset = (
        given[None, :] - asking[:, None] + slot_count + slot_count // 2
    ) % slot_count - slot_count // 2
    reached = position[:, None] + offset
    valid = (
        (jnp.abs(offset) <= jnp.minimum(width, REACH)[:, None])
        & (reached >= 0)
        & (reached < slot_count)
    )
    valid = valid.astype(jnp.int32).reshape(12)

    value = {"k": keys, "v": values, "q": query}
    held = {"spatial": None, "result": None}

    def permute(name, source, where_to):
        value[name] = moved(value[source], "queue", where_to)

    def packed(indices):
        outs = pack(core, keys, values, [CHUNKS[i] for i in indices])
        for n, i in enumerate(indices):
            value[f"A{i}"], value[f"X{i}"] = outs[2 * n], outs[2 * n + 1]

    def emit(name):
        kind = name[:2]
        at = int(name[2:].split("_")[0] or 0)
        if kind == "pk":
            first, last = (int(n) for n in name[2:].split("_"))
            packed(range(first, last))
        elif kind in ("ek", "ev", "eq"):
            permute(kind, kind[1], other_core)
        elif kind == "fa":
            permute(f"1a{at}", f"A{at}", pair_chip)
        elif kind == "fx":
            permute(f"1x{at}", f"X{at}", pair_chip_other_core)
        elif kind in ("sa", "sx"):
            permute(f"2{kind[1]}{at}", f"1{kind[1]}{at}", onward)
        elif kind == "sp":
            held["spatial"] = spatial(
                level, query, keys, values, gate_table,
                sum(HEAD_RUNS[:at]), HEAD_RUNS[at], held["spatial"],
            )
        elif kind == "te":
            group = GROUPS[at]
            frames = [value[f"{n}{i}"] for i in group for n in ("1a", "1x", "2a", "2x")]
            value[f"K{at}"], value[f"S{at}"] = temporal(
                valid, core, (query, keys, values), (value["eq"], value["ek"], value["ev"]),
                frames, [CHUNKS[i] for i in group],
            )
        elif kind == "re":
            permute(f"R{at}", f"S{at}", other_core)
        elif kind == "bl":
            first, last = (int(n) for n in name[2:].split("_"))
            halves = [value[f"{n}{i}"] for i in range(first, last) for n in "KR"]
            held["result"] = blend(
                core, level, gate_table, halves, held["spatial"], held["result"],
                [
                    (CHUNKS[GROUPS[i][0]][0], sum(CHUNKS[n][1] for n in GROUPS[i]))
                    for i in range(first, last)
                ],
            )

    for name in PLAN:
        emit(name)
    return held["result"]


PLAN = [
    *("pk0_1", "fa0", "fx0", "ek", "ev", "eq", "pk1_13"),
    *("sa0", "fa1", "fx1", "fa2", "fx2"),
    *("sx0", "fa3", "fx3", "fa4", "fx4"),
    *("sa1", "fa5", "fx5", "fa6", "fx6"),
    *("sx1", "fa7", "fx7", "fa8", "fx8"),
    *("sa2", "fa9", "fx9", "fa10", "fx10"),
    *("sx2", "fa11", "fx11", "fa12", "fx12"),
    *("sa3", "te0", "re0"),
    *("sx3", "te1", "re1", "sa4", "sp0"),
    *("sx4", "sp1", "sa5", "sp2"),
    *("sx5", "te2", "re2", "sa6", "sp3"),
    *("sx6", "sp4", "sa7", "sp5"),
    *("sx7", "te3", "re3", "sa8", "sp6"),
    *("sx8", "sp7", "sa9", "sp8"),
    *("sx9", "te4", "re4", "sa10", "sp9"),
    *("sx10", "bl0_1", "bl1_4", "sa11", "sx11", "sa12"),
    *("te5", "re5", "sx12", "te6", "re6"),
    *("bl4_6", "te7", "re7", "bl6_7", "bl7_8"),
]


def solution(mesh):
    in_specs = (
        P(("groups", "queue"), None, None),
        P(("groups", "queue"), None, None),
        P(("groups", "queue"), None, None),
        P(),
        P("groups"),
        P("groups"),
        P("groups"),
    )
    out_specs = P(("groups", "queue"), None, None)

    return jax.shard_map(body, mesh=mesh, in_specs=in_specs, out_specs=out_specs, check_vma=False)
```

```python
import functools
import math

import jax
import jax.numpy as jnp
from jax import lax
from jax.experimental import pallas as pl
from jax.experimental.pallas import tpu as pltpu
from jax.sharding import PartitionSpec as P


HEAD_DIM = 128
REACH = 2
CALL_VMEM = 12 << 20
SCALE = 1.0 / math.sqrt(HEAD_DIM)
LOG2_E = math.log2(math.e)
SPATIAL_ROWS = 384
CHUNKS = [(640, 64)] + [(64 * i, 64) for i in range(10)] + [(720, 48), (704, 16)]
GROUPS = [[0], [1, 2], [3, 4], [5, 6], [7, 8], [9, 10], [11], [12]]
HEAD_RUNS = [2] * 10


def moved(value, axis, where_to):
    count = lax.axis_size(axis)
    return lax.ppermute(value, axis, [(source, where_to(source) % count) for source in range(count)])


def other_core(index):
    return index ^ 1


def pair_chip(index):
    return index ^ 2


def pair_chip_other_core(index):
    return index ^ 3


def onward(index):
    return index - 4 if index & 2 else index + 4


def pack_kernel(chunks, core_ref, k_ref, v_ref, *refs):
    count = len(chunks)
    outs, held, read_sem, write_sem = refs[: 2 * count], refs[-3], refs[-2], refs[-1]
    half = k_ref.shape[1] // 2
    core = core_ref[0]

    def reads(i, side):
        low, rows = chunks[i]
        at = sum(n for _, n in chunks[:i])
        from_column = pl.multiple_of((core if side == 0 else 1 - core) * half, half)
        return [
            pltpu.make_async_copy(
                source.at[pl.ds(low, rows), pl.ds(from_column, half)],
                held.at[side, plane, pl.ds(at, rows), :],
                read_sem.at[2 * i + side, plane],
            )
            for plane, source in enumerate((k_ref, v_ref))
        ]

    def write(i, side):
        rows = chunks[i][1]
        at = sum(n for _, n in chunks[:i])
        return pltpu.make_async_copy(
            held.at[side, :, pl.ds(at, rows), :], outs[2 * i + side], write_sem.at[2 * i + side]
        )

    pieces = [(i, side) for i in range(count) for side in range(2)]
    for piece in pieces:
        for copy in reads(*piece):
            copy.start()
    for piece in pieces:
        for copy in reads(*piece):
            copy.wait()
        write(*piece).start()
    for piece in pieces:
        write(*piece).wait()


def pack(core, keys, values, chunks):
    half = keys.shape[1] // 2
    total = sum(rows for _, rows in chunks)
    anywhere = pl.BlockSpec(memory_space=pl.ANY)
    return pl.pallas_call(
        functools.partial(pack_kernel, chunks),
        grid_spec=pltpu.PrefetchScalarGridSpec(
            num_scalar_prefetch=1,
            grid=(1,),
            in_specs=[anywhere, anywhere],
            out_specs=[anywhere] * (2 * len(chunks)),
            scratch_shapes=[
                pltpu.VMEM((2, 2, total, half), keys.dtype),
                pltpu.SemaphoreType.DMA((2 * len(chunks), 2)),
                pltpu.SemaphoreType.DMA((2 * len(chunks),)),
            ],
        ),
        out_shape=[
            jax.ShapeDtypeStruct((2, rows, half), keys.dtype) for _, rows in chunks for _ in range(2)
        ],
        cost_estimate=pl.CostEstimate(
            flops=0, bytes_accessed=16 * total * half, transcendentals=0
        ),
        name="pack",
    )(core, keys, values)


def spatial_kernel(level_ref, q_ref, k_ref, v_ref, gate_ref, *refs):
    o_ref = refs[-1]
    tokens = q_ref.shape[0]
    step = math.gcd(tokens, SPATIAL_ROWS)
    k = k_ref[...]
    v = v_ref[...]
    gate = gate_ref[0, 0:1, :]
    for at in range(0, tokens, step):
        scores = lax.dot_general(
            q_ref[at : at + step, :],
            k,
            (((1,), (1,)), ((), ())),
            preferred_element_type=jnp.float32,
        )
        expd = jnp.exp2((scores - jnp.max(scores, axis=-1, keepdims=True)) * (SCALE * LOG2_E))
        total = jnp.sum(expd, axis=-1, keepdims=True)
        mixed = lax.dot_general(
            expd.astype(jnp.bfloat16),
            v,
            (((1,), (0,)), ((), ())),
            preferred_element_type=jnp.float32,
        )
        o_ref[at : at + step, :] = mixed * (gate * (1.0 / total))


def spatial(level, query, keys, values, gate_table, first, heads, held):
    tokens, width = query.shape
    col = pl.BlockSpec((tokens, HEAD_DIM), lambda h, lv: (0, first + h))
    in_specs = [
        col,
        col,
        col,
        pl.BlockSpec((1, 2, HEAD_DIM), lambda h, lv: (lv[0], 0, first + h)),
    ]
    operands = [level, query, keys, values, gate_table]
    aliases = {}
    if held is not None:
        in_specs.append(pl.BlockSpec(memory_space=pl.ANY))
        aliases = {len(operands): 0}
        operands.append(held)
    return pl.pallas_call(
        spatial_kernel,
        grid_spec=pltpu.PrefetchScalarGridSpec(
            num_scalar_prefetch=1,
            grid=(heads,),
            in_specs=in_specs,
            out_specs=col,
        ),
        out_shape=jax.ShapeDtypeStruct((tokens, width), jnp.float32),
        input_output_aliases=aliases,
        cost_estimate=pl.CostEstimate(
            flops=4 * heads * tokens * tokens * HEAD_DIM,
            bytes_accessed=10 * tokens * heads * HEAD_DIM,
            transcendentals=heads * tokens * tokens,
        ),
        compiler_params=pltpu.CompilerParams(vmem_limit_bytes=CALL_VMEM),
        name="spatial",
    )(*operands)


def temporal_kernel(sizes, valid_ref, core_ref, *refs):
    qa_ref, ka_ref, va_ref, qb_ref, kb_ref, vb_ref = refs[:6]
    outs = refs[-2:]
    width = qa_ref.shape[1]
    step = 16
    for at in range(0, width, HEAD_DIM):
        span = slice(at, at + HEAD_DIM)
        start = 0
        for piece, rows in enumerate(sizes):
            frames = refs[6 + 4 * piece : 10 + 4 * piece]
            for low in range(0, rows, step):
                inner = slice(low, low + step)
                part = slice(start + low, start + low + step)
                near_keys = [r[part, span] for r in (ka_ref, kb_ref)]
                near_keys += [f[0, inner, span] for f in frames]
                near_values = [r[part, span] for r in (va_ref, vb_ref)]
                near_values += [f[1, inner, span] for f in frames]
                near_keys = [x.astype(jnp.float32) for x in near_keys]
                for which, q_ref in enumerate((qa_ref, qb_ref)):
                    q = q_ref[part, span].astype(jnp.float32) * (SCALE * LOG2_E)
                    scores = []
                    for f in range(6):
                        score = jnp.sum(q * near_keys[f], axis=-1, keepdims=True)
                        score = jnp.broadcast_to(score, q.shape)
                        scores.append(jnp.where(valid_ref[which * 6 + f] > 0, score, -1e30))
                    top = functools.reduce(jnp.maximum, scores)
                    expd = [jnp.exp2(s - top) for s in scores]
                    total = functools.reduce(jnp.add, expd)
                    mixed = functools.reduce(
                        jnp.add, [expd[f] * near_values[f].astype(jnp.float32) for f in range(6)]
                    )
                    outs[which][part, span] = (mixed * (1.0 / total)).astype(jnp.bfloat16)
            start += rows


def temporal(valid, core, own, partner, frames, chunks):
    low = chunks[0][0]
    sizes = [n for _, n in chunks]
    rows = sum(sizes)
    half = own[0].shape[1] // 2
    steps = 2 if rows > 32 else 1
    width = half // steps
    at = low // rows
    mine = pl.BlockSpec((rows, width), lambda i, va, c: (at, steps * c[0] + i))
    frame_specs = [pl.BlockSpec((2, n, width), lambda i, va, c: (0, 0, i)) for n in sizes]
    out = pl.BlockSpec((rows, width), lambda i, va, c: (0, i))
    shape = jax.ShapeDtypeStruct((rows, half), jnp.bfloat16)
    return pl.pallas_call(
        functools.partial(temporal_kernel, sizes),
        grid_spec=pltpu.PrefetchScalarGridSpec(
            num_scalar_prefetch=2,
            grid=(steps,),
            in_specs=[mine] * 6 + [spec for spec in frame_specs for _ in range(4)],
            out_specs=[out, out],
        ),
        out_shape=[shape, shape],
        cost_estimate=pl.CostEstimate(
            flops=72 * rows * half, bytes_accessed=32 * rows * half, transcendentals=12 * rows * half
        ),
        compiler_params=pltpu.CompilerParams(vmem_limit_bytes=CALL_VMEM),
        name="temporal",
    )(valid, core, *own, *partner, *frames)


def blend_kernel(count, core_ref, level_ref, gate_ref, part_ref, *refs):
    o_ref = refs[-1]
    core = core_ref[0]
    half = part_ref.shape[1] // 2

    def piece(mine_ref, other_ref):
        for side in range(2):
            span = slice(side * half, (side + 1) * half)
            temporal_part = jnp.where(core == side, mine_ref[...], other_ref[...])
            o_ref[0, :, span] = (
                part_ref[:, span] + gate_ref[0, 1:2, span] * temporal_part.astype(jnp.float32)
            ).astype(o_ref.dtype)

    if count == 1:
        piece(refs[0], refs[1])
    else:
        for i in range(count):
            pl.when(pl.program_id(0) == i)(functools.partial(piece, refs[2 * i], refs[2 * i + 1]))


def blend(core, level, gate_table, halves, part, held, chunks):
    tokens, width = part.shape
    low, rows = chunks[0]
    at = low // rows
    count = len(chunks)
    piece = pl.BlockSpec((rows, width // 2), lambda i, c, lv: (0, 0))
    in_specs = [
        pl.BlockSpec((1, 2, width), lambda i, c, lv: (lv[0], 0, 0)),
        pl.BlockSpec((rows, width), lambda i, c, lv: (at + i, 0)),
    ] + [piece] * (2 * count)
    operands = [core, level, gate_table, part] + list(halves)
    aliases = {}
    if held is not None:
        in_specs.append(pl.BlockSpec(memory_space=pl.ANY))
        aliases = {len(operands): 0}
        operands.append(held)
    return pl.pallas_call(
        functools.partial(blend_kernel, count),
        grid_spec=pltpu.PrefetchScalarGridSpec(
            num_scalar_prefetch=2,
            grid=(count,),
            in_specs=in_specs,
            out_specs=pl.BlockSpec((1, rows, width), lambda i, c, lv: (0, at + i, 0)),
        ),
        out_shape=jax.ShapeDtypeStruct((1, tokens, width), jnp.bfloat16),
        input_output_aliases=aliases,
        cost_estimate=pl.CostEstimate(
            flops=2 * count * rows * width,
            bytes_accessed=8 * count * rows * width,
            transcendentals=0,
        ),
        compiler_params=pltpu.CompilerParams(vmem_limit_bytes=CALL_VMEM),
        name="blend",
    )(*operands)


def body(query, keys, values, gate_table, levels, window, queue_head):
    query, keys, values = (
        pltpu.with_memory_space_constraint(x[0], pltpu.HBM) for x in (query, keys, values)
    )
    slot_count = lax.axis_size("queue")
    own = lax.axis_index("queue")
    core = (own & 1).astype(jnp.int32).reshape(1)

    slot_ids = jnp.arange(slot_count, dtype=jnp.int32)
    level = jnp.sum(jnp.where(slot_ids == own, levels, 0)).reshape(1)
    far = jnp.where(own & 2, own + 2, own - 2 + slot_count) % slot_count
    asking = jnp.stack([own, own ^ 1])
    given = jnp.stack([own, own ^ 1, own ^ 2, own ^ 3, far, far ^ 1])
    width = jnp.sum(jnp.where(slot_ids[None, :] == asking[:, None], window[None, :], 0), axis=1)
    position = (asking - queue_head[0]) % slot_count
    offset = (
        given[None, :] - asking[:, None] + slot_count + slot_count // 2
    ) % slot_count - slot_count // 2
    reached = position[:, None] + offset
    valid = (
        (jnp.abs(offset) <= jnp.minimum(width, REACH)[:, None])
        & (reached >= 0)
        & (reached < slot_count)
    )
    valid = valid.astype(jnp.int32).reshape(12)

    value = {"k": keys, "v": values, "q": query}
    held = {"spatial": None, "result": None}

    def permute(name, source, where_to):
        value[name] = moved(value[source], "queue", where_to)

    def packed(indices):
        outs = pack(core, keys, values, [CHUNKS[i] for i in indices])
        for n, i in enumerate(indices):
            value[f"A{i}"], value[f"X{i}"] = outs[2 * n], outs[2 * n + 1]

    def emit(name):
        kind = name[:2]
        at = int(name[2:].split("_")[0] or 0)
        if kind == "pk":
            first, last = (int(n) for n in name[2:].split("_"))
            packed(range(first, last))
        elif kind in ("ek", "ev", "eq"):
            permute(kind, kind[1], other_core)
        elif kind == "fa":
            permute(f"1a{at}", f"A{at}", pair_chip)
        elif kind == "fx":
            permute(f"1x{at}", f"X{at}", pair_chip_other_core)
        elif kind in ("sa", "sx"):
            permute(f"2{kind[1]}{at}", f"1{kind[1]}{at}", onward)
        elif kind == "sp":
            held["spatial"] = spatial(
                level, query, keys, values, gate_table,
                sum(HEAD_RUNS[:at]), HEAD_RUNS[at], held["spatial"],
            )
        elif kind == "te":
            group = GROUPS[at]
            frames = [value[f"{n}{i}"] for i in group for n in ("1a", "1x", "2a", "2x")]
            value[f"K{at}"], value[f"S{at}"] = temporal(
                valid, core, (query, keys, values), (value["eq"], value["ek"], value["ev"]),
                frames, [CHUNKS[i] for i in group],
            )
        elif kind == "re":
            permute(f"R{at}", f"S{at}", other_core)
        elif kind == "bl":
            first, last = (int(n) for n in name[2:].split("_"))
            halves = [value[f"{n}{i}"] for i in range(first, last) for n in "KR"]
            held["result"] = blend(
                core, level, gate_table, halves, held["spatial"], held["result"],
                [
                    (CHUNKS[GROUPS[i][0]][0], sum(CHUNKS[n][1] for n in GROUPS[i]))
                    for i in range(first, last)
                ],
            )

    for name in PLAN:
        emit(name)
    return held["result"]


PLAN = [
    *("pk0_1", "fa0", "fx0", "ek", "ev", "eq", "pk1_13"),
    *("sa0", "fa1", "fx1", "fa2", "fx2"),
    *("sx0", "fa3", "fx3", "fa4", "fx4"),
    *("sa1", "fa5", "fx5", "fa6", "fx6"),
    *("sx1", "fa7", "fx7", "fa8", "fx8"),
    *("sa2", "fa9", "fx9", "fa10", "fx10"),
    *("sx2", "fa11", "fx11", "fa12", "fx12"),
    *("sa3", "te0", "re0"),
    *("sx3", "te1", "re1", "sa4", "sp0"),
    *("sx4", "sp1", "sa5", "sp2"),
    *("sx5", "te2", "re2", "sa6", "sp3"),
    *("sx6", "sp4", "sa7", "sp5"),
    *("sx7", "te3", "re3", "sa8", "sp6"),
    *("sx8", "sp7", "sa9", "sp8"),
    *("sx9", "te4", "re4", "sa10", "sp9"),
    *("sx10", "bl0_1", "bl1_4", "sa11", "sx11", "sa12"),
    *("te5", "re5", "sx12", "bl4_6", "te6", "re6"),
    *("te7", "re7", "bl6_7", "bl7_8"),
]


def solution(mesh):
    in_specs = (
        P(("groups", "queue"), None, None),
        P(("groups", "queue"), None, None),
        P(("groups", "queue"), None, None),
        P(),
        P("groups"),
        P("groups"),
        P("groups"),
    )
    out_specs = P(("groups", "queue"), None, None)

    return jax.shard_map(body, mesh=mesh, in_specs=in_specs, out_specs=out_specs, check_vma=False)
```
